32 devices in a mesh: member: 16 (over z, y, x), domain: 1, group: 2 (over core).
Axes of the slice: x: 2, y: 2, z: 4, core: 2. Of those that a mesh axis runs over, the one named last changes fastest.
Arguments:
- ensemble: float32 [128, 3, 8, 512], P(('member', 'group'), None, 'domain'), may hold values from -1 to 1
- obs_cell: int32 [1, 32, 128], P('domain', ('member', 'group')), may hold values from 0 to 383
- obs_value: float32 [1, 32, 128], P('domain', ('member', 'group')), may hold values from -1.5 to 1.5
- obs_rinv: float32 [1, 32, 128], P('domain', ('member', 'group')), may hold values from 100 to 1600
- obs_live: int32 [1, 32, 128], P('domain', ('member', 'group')), may hold values 0 or 1
Outputs:
- analysed: float32 [128, 3, 8, 512], P(('member', 'group'), None, 'domain')
The draws below stay inside these ranges and needn't reach their ends.
All inputs are finite; a program needn't handle non-finite values. Where the reference program divides by a largest or mean magnitude, that divisor is 1e-20 or more. No bound on the sum of `obs_live` on one device may be relied on, other than what follows from the above.
Results may differ from the reference program's by a relative error of at most 0.00017.
Values sent between devices are 32-bit elements; how exact they have to be, the bound alone decides.
A program may use at most 64 MiB of HBM per device.

```python
import math
import jax
import jax.numpy as jnp
from jax import lax

MEM_DEV = 4
MEMBERS = 128
ROWS = 8
PCOL = 16
MESH_POINTS_EAST = 512
MESH_POINTS_NORTH = 8
PY = 1
PX = 32
CELLS = 384
OBS = 128
STEPS = 8
NS_ITERS = 5


def touch_ends(values, rng, low, largest):
    dims = values.shape
    place = [jax.random.randint(jax.random.fold_in(rng, axis), (), 0, dims[axis]) for axis in range(len(dims))]
    values = values.at[tuple(place)].set(low)
    longest = dims.index(max(dims))
    place[longest] = (place[longest] + 1) % dims[longest]
    return values.at[tuple(place)].set(largest)


def block_scale(rng, extent, shards, least, largest):
    loudness, own = 1.0, jax.random.fold_in(rng, 6)
    for position, blocks in shards:
        heights = jnp.exp(jax.random.uniform(jax.random.fold_in(own, position), (blocks,), jnp.float32, least / len(shards), largest / len(shards)))
        loudness = loudness * jnp.repeat(heights, extent[position] // blocks).reshape([-1 if axis == position else 1 for axis in range(len(extent))])
    return loudness


def gaussian(stream_key, shape, width, bound, shards=(), kind=jnp.bfloat16):
    loudness = block_scale(stream_key, shape, shards, -0.22, 0.18) if shards else 1.0
    drawn = jax.random.normal(stream_key, shape, jnp.float32) * width * loudness
    return jnp.minimum(jnp.maximum(drawn, -bound), bound).astype(kind)


def setup_inputs(seed: int = 0) -> dict:
    splits = jax.random.split(jax.random.key(seed), 6)
    ensemble = gaussian(splits[0], (MEMBERS, 3, MESH_POINTS_NORTH, MESH_POINTS_EAST), 0.25, 1.0, ((0, 32),), jnp.float32)
    obs_cell = touch_ends(jax.random.randint(splits[1], (PY, PX, OBS), 0, CELLS), jax.random.fold_in(splits[1], 1), 0, CELLS - 1).astype(jnp.int32)
    obs_value = gaussian(splits[2], (PY, PX, OBS), 0.3, 1.5, ((1, 32),), jnp.float32)
    obs_rinv = jnp.clip(jnp.exp(math.log(1600.0) - 2.7725887 * jax.random.uniform(splits[3], (PY, PX, OBS), jnp.float32) ** block_scale(splits[3], (PY, PX, OBS), ((1, 32),), -0.2, 0.2)), 100.0, 1600.0)
    obs_live = touch_ends((jax.random.randint(splits[4], (PY, PX, OBS), 0, 4) < 3).astype(jnp.int32), jax.random.fold_in(splits[4], 1), 0, 1)
    return dict(ensemble=ensemble, obs_cell=obs_cell, obs_value=obs_value, obs_rinv=obs_rinv, obs_live=obs_live)


HIGH = lax.Precision.HIGHEST

def split_parts(values):
    centre = values[:, 1:-1]
    north = values[:, 2:]
    south = values[:, :-2]
    east = jnp.roll(centre, -1, axis=-1)
    west = jnp.roll(centre, 1, axis=-1)
    return (0.25 * (north + south + east + west), 0.5 * (east - west), 0.5 * (north - south), centre)

def advance(padded):
    height = padded[:, 0]
    speed_u = padded[:, 1]
    speed_v = padded[:, 2]
    depth = 1.0 + height
    h_avg, h_dx, h_dy, h_mid = split_parts(height)
    u_avg, u_dx, u_dy, u_mid = split_parts(speed_u)
    v_avg, v_dx, v_dy, v_mid = split_parts(speed_v)
    flux_x = split_parts(depth * speed_u)[1]
    flux_y = split_parts(depth * speed_v)[2]
    new_h = h_avg - 0.3 * (flux_x + flux_y)
    new_u = u_avg - 0.3 * (u_mid * u_dx + v_mid * u_dy + h_dx - 0.2 * v_mid)
    new_v = v_avg - 0.3 * (u_mid * v_dx + v_mid * v_dy + h_dy + 0.2 * u_mid)
    return jnp.stack([new_h, new_u, new_v], axis=1)

def predict_domain_piece(domain_piece):
    for turn_index in range(STEPS):
        padded = jnp.pad(domain_piece, ((0, 0), (0, 0), (1, 1), (0, 0)))
        domain_piece = advance(padded)
    return domain_piece

def analyse(inputs):
    states, nearby = inputs
    ensemble_size = states.shape[0]
    centre_row = lax.optimization_barrier(jnp.mean(states, axis=0))
    anomaly = states - centre_row
    slots = nearby.shape[1] // 3
    offset = (jnp.arange(3 * slots) // slots - 1).astype(jnp.float32)
    dist_y = offset * ROWS + nearby[ensemble_size + 2] - 0.5 * (ROWS - 1)
    taper = jnp.exp(-0.5 * (dist_y / ROWS) * (dist_y / ROWS))
    weights = nearby[ensemble_size + 1] * taper
    innov = nearby[ensemble_size]
    seen = nearby[:ensemble_size]
    gram = jnp.dot(seen * weights[None, :], seen.T, precision=HIGH)
    ident = jnp.eye(ensemble_size, dtype=jnp.float32)
    system = (ensemble_size - 1) / 1.1 * ident + gram
    norm_c = jnp.max(lax.optimization_barrier(jnp.sum(jnp.abs(system), axis=1)))
    root_m = system / norm_c
    inverse = ident
    for turn_index in range(NS_ITERS):
        factor = 1.5 * ident - 0.5 * jnp.dot(inverse, root_m, precision=HIGH)
        root_m = jnp.dot(root_m, factor, precision=HIGH)
        inverse = jnp.dot(factor, inverse, precision=HIGH)
    inverse = inverse / jnp.sqrt(norm_c)
    pushed = jnp.dot(seen, weights * innov, precision=HIGH)
    shift_w = jnp.dot(inverse, jnp.dot(inverse, pushed, precision=HIGH), precision=HIGH)
    mixing = math.sqrt(ensemble_size - 1) * inverse + shift_w[:, None]
    return centre_row + lax.dot_general(mixing, anomaly, (((0,), (0,)), ((), ())), precision=HIGH)

def reference(ensemble, obs_cell, obs_value, obs_rinv, obs_live):
    ensemble_size = ensemble.shape[0]
    domain_pieces = ensemble.reshape(ensemble_size // MEM_DEV, MEM_DEV, 3, MESH_POINTS_NORTH, MESH_POINTS_EAST)
    physical_fields_vector = lax.map(predict_domain_piece, domain_pieces).reshape(ensemble_size, 3, MESH_POINTS_NORTH, MESH_POINTS_EAST)
    patches = physical_fields_vector.reshape(ensemble_size, 3, PY, ROWS, PX, PCOL).transpose(2, 4, 0, 1, 3, 5).reshape(PY, PX, ensemble_size, CELLS)
    index = jnp.broadcast_to(obs_cell[:, :, None, :], (PY, PX, ensemble_size, OBS))
    seen_all = jnp.take_along_axis(patches, index, axis=3)
    seen_mean = lax.optimization_barrier(jnp.mean(seen_all, axis=2))
    seen_anom = seen_all - seen_mean[:, :, None, :]
    innov = obs_value - seen_mean
    weight = obs_rinv * obs_live.astype(jnp.float32)
    obs_row = (obs_cell % (ROWS * PCOL) // PCOL).astype(jnp.float32)
    packed = jnp.concatenate([seen_anom, innov[:, :, None, :], weight[:, :, None, :], obs_row[:, :, None, :]], axis=2)
    padded = jnp.pad(packed, ((1, 1), (0, 0), (0, 0), (0, 0)))
    nearby = jnp.stack([padded[:-2], padded[1:-1], padded[2:]], axis=3).reshape(PY * PX, ensemble_size + 3, 3 * OBS)
    done = lax.map(analyse, (patches.reshape(PY * PX, ensemble_size, CELLS), nearby))
    done = done.reshape(PY, PX, ensemble_size, 3, ROWS, PCOL).transpose(2, 3, 0, 4, 1, 5)
    return done.reshape(ensemble_size, 3, MESH_POINTS_NORTH, MESH_POINTS_EAST)
```

```python
import functools
import math

import jax
import jax.numpy as jnp
from jax import lax
from jax.experimental import pallas as pl
from jax.experimental.pallas import tpu as pltpu
from jax.sharding import PartitionSpec as P

PCOL = 16
STEPS = 8
DEEP = 4
NS_ITERS = 5


HIGH = lax.Precision.HIGHEST


def with_halo(block, sides, width):
    for axis, dim in sides:
        count = lax.axis_size(axis)
        forward = [(i, i + 1) for i in range(count - 1)]
        backward = [(target, source) for source, target in forward]
        low = lax.ppermute(
            lax.slice_in_dim(block, block.shape[dim] - width, None, axis=dim), axis, forward
        )
        high = lax.ppermute(lax.slice_in_dim(block, 0, width, axis=dim), axis, backward)
        block = jnp.concatenate([low, block, high], axis=dim)
    return block


def split_parts(values):
    centre = values[:, 1:-1]
    north = values[:, 2:]
    south = values[:, :-2]
    east = jnp.roll(centre, -1, axis=-1)
    west = jnp.roll(centre, 1, axis=-1)
    return (
        0.25 * (north + south + east + west),
        0.5 * (east - west),
        0.5 * (north - south),
        centre,
    )


def advance(padded):
    height = padded[:, 0]
    speed_u = padded[:, 1]
    speed_v = padded[:, 2]
    depth = 1.0 + height
    h_avg, h_dx, h_dy, h_mid = split_parts(height)
    u_avg, u_dx, u_dy, u_mid = split_parts(speed_u)
    v_avg, v_dx, v_dy, v_mid = split_parts(speed_v)
    flux_x = split_parts(depth * speed_u)[1]
    flux_y = split_parts(depth * speed_v)[2]
    new_h = h_avg - 0.3 * (flux_x + flux_y)
    new_u = u_avg - 0.3 * (u_mid * u_dx + v_mid * u_dy + h_dx - 0.2 * v_mid)
    new_v = v_avg - 0.3 * (u_mid * v_dx + v_mid * v_dy + h_dy + 0.2 * u_mid)
    return jnp.stack([new_h, new_u, new_v], axis=1)


def local(ensemble, obs_cell, obs_value, obs_rinv, obs_live):
    physical_fields_vector = ensemble
    mem_local = physical_fields_vector.shape[0]
    rows = physical_fields_vector.shape[2]
    width_x = physical_fields_vector.shape[3]
    strip = lax.axis_index("domain")
    total_rows = rows * lax.axis_size("domain")
    for block_index in range(STEPS // DEEP):
        padded = with_halo(physical_fields_vector, (("domain", 2),), DEEP)
        for sub_index in range(DEEP):
            padded = advance(padded)
            if sub_index + 1 < DEEP:
                margin = DEEP - 1 - sub_index
                global_row = strip * rows - margin + jnp.arange(padded.shape[2])
                inside = (global_row >= 0) & (global_row < total_rows)
                padded = jnp.where(inside[None, None, :, None], padded, 0.0)
        physical_fields_vector = padded
    domain_pieces = width_x // PCOL
    cells = 3 * rows * PCOL
    pieces = (
        physical_fields_vector.reshape(mem_local, 3, rows, domain_pieces, PCOL)
        .transpose(0, 3, 1, 2, 4)
        .reshape(mem_local, domain_pieces, cells)
    )
    gathered = lax.all_to_all(pieces, ("member", "group"), split_axis=1, concat_axis=0, tiled=True)
    members = gathered.reshape(-1, cells)
    ensemble_size = members.shape[0]
    centre_row = jnp.mean(members, axis=0)
    anomaly = members - centre_row
    picker = (obs_cell[0, 0][None, :] == jnp.arange(cells)[:, None]).astype(jnp.float32)
    seen = jnp.dot(anomaly, picker, precision=HIGH)
    seen_mean = jnp.dot(centre_row[None, :], picker, precision=HIGH)[0]
    innov = obs_value[0, 0] - seen_mean
    weight = obs_rinv[0, 0] * obs_live[0, 0].astype(jnp.float32)
    obs_row = (obs_cell[0, 0] % (rows * PCOL) // PCOL).astype(jnp.float32)
    packed = jnp.concatenate([seen, innov[None, :], weight[None, :], obs_row[None, :]], axis=0)[
        :, None, :
    ]
    nearby = with_halo(packed, (("domain", 1),), 1)
    slots = packed.shape[2]
    nearby = nearby.reshape(ensemble_size + 3, 3 * slots)
    offset = (jnp.arange(3 * slots) // slots - 1).astype(jnp.float32)
    dist_y = offset * rows + nearby[ensemble_size + 2] - 0.5 * (rows - 1)
    taper = jnp.exp(-0.5 * (dist_y / rows) * (dist_y / rows))
    weights = nearby[ensemble_size + 1] * taper
    seen_all = nearby[:ensemble_size]
    gram = jnp.dot(seen_all * weights[None, :], seen_all.T, precision=HIGH)
    ident = jnp.eye(ensemble_size, dtype=jnp.float32)
    system = (ensemble_size - 1) / 1.1 * ident + gram
    norm_c = jnp.max(jnp.sum(jnp.abs(system), axis=1))
    root_m = system / norm_c
    inverse = ident
    for turn_index in range(NS_ITERS):
        factor = 1.5 * ident - 0.5 * jnp.dot(inverse, root_m, precision=HIGH)
        if turn_index + 1 < NS_ITERS:
            root_m = jnp.dot(root_m, factor, precision=HIGH)
        inverse = jnp.dot(factor, inverse, precision=HIGH)
    inverse = inverse / jnp.sqrt(norm_c)
    pushed = jnp.dot(seen_all, weights * nearby[ensemble_size], precision=HIGH)
    shift_w = jnp.dot(inverse, jnp.dot(inverse, pushed, precision=HIGH), precision=HIGH)
    mixing = math.sqrt(ensemble_size - 1) * inverse + shift_w[:, None]
    result = centre_row + lax.dot_general(mixing, anomaly, (((0,), (0,)), ((), ())), precision=HIGH)
    returned = lax.all_to_all(
        result.reshape(ensemble_size, 1, cells),
        ("member", "group"),
        split_axis=0,
        concat_axis=1,
        tiled=True,
    )
    return (
        returned.reshape(mem_local, domain_pieces, 3, rows, PCOL)
        .transpose(0, 2, 3, 1, 4)
        .reshape(mem_local, 3, rows, width_x)
    )


def swap_groups(x, row, group):
    for d in (4, 2, 1):
        row_bit = (row // d) % 2
        group_bit = (group // d) % 2
        up = pltpu.roll(pltpu.roll(x, 8 - d, 0), 16 * d, 1)
        if d == 4:
            other = up
        else:
            down = pltpu.roll(pltpu.roll(x, d, 0), 128 - 16 * d, 1)
            other = jnp.where(group_bit == 1, up, down)
        x = jnp.where(row_bit == group_bit, x, other)
    return x


def swap_members(blocks, row):
    blocks = list(blocks)
    for d in (2, 1):
        low = (row // d) % 2 == 0
        for i in range(4):
            if (i // d) % 2 == 0:
                a, b = blocks[i], blocks[i + d]
                blocks[i] = jnp.where(low, a, pltpu.roll(b, d, 0))
                blocks[i + d] = jnp.where(low, pltpu.roll(a, 8 - d, 0), b)
    return blocks


def forecast_step(fields):
    h, u, v = fields
    width = h.shape[1]
    row = lax.broadcasted_iota(jnp.int32, h.shape, 0)
    first, last = row == 0, row == h.shape[0] - 1

    def around(x):
        return (
            pltpu.roll(x, width - 1, 1),
            pltpu.roll(x, 1, 1),
            jnp.where(last, 0.0, pltpu.roll(x, x.shape[0] - 1, 0)),
            jnp.where(first, 0.0, pltpu.roll(x, 1, 0)),
        )

    he, hw, hn, hs = around(h)
    ue, uw, un, us = around(u)
    ve, vw, vn, vs = around(v)
    flux = ((1.0 + he) * ue - (1.0 + hw) * uw) + ((1.0 + hn) * vn - (1.0 + hs) * vs)
    new_h = 0.25 * ((hn + hs) + (he + hw)) - 0.15 * flux
    new_u = 0.25 * ((un + us) + (ue + uw)) - 0.15 * (u * (ue - uw) + v * (un - us) + (he - hw)) + 0.06 * v
    new_v = 0.25 * ((vn + vs) + (ve + vw)) - 0.15 * (u * (ve - vw) + v * (vn - vs) + (hn - hs)) - 0.06 * u
    return new_h, new_u, new_v


def halves(x):
    hi = x.astype(jnp.bfloat16)
    lo = (x - hi.astype(jnp.float32)).astype(jnp.bfloat16)
    return hi, lo


def left_of(x):
    return jnp.concatenate(halves(x), axis=1)


def right_of(x):
    wide = jnp.concatenate(halves(x), axis=1)
    return jnp.concatenate([wide, wide], axis=0)


def product(left, right):
    both = jnp.dot(left, right, preferred_element_type=jnp.float32)
    half = both.shape[1] // 2
    return both[:, :half] + both[:, half:]


def fused(
    devices,
    cores,
    ens_ref,
    cell_ref,
    value_ref,
    rinv_ref,
    live_ref,
    out_ref,
    send,
    recv,
    back_send,
    back_recv,
    sems,
):
    members = devices * 4
    me = lax.axis_index("member") * cores + lax.axis_index("group")

    def device_of(k):
        target = lax.rem(me + k, devices)
        return target, {"member": target // cores, "group": lax.rem(target, cores)}

    barrier = pltpu.get_barrier_semaphore()

    def greet(i, carry):
        _, where = device_of(i + 1)
        pl.semaphore_signal(barrier, inc=1, device_id=where, device_id_type=pl.DeviceIdType.MESH)
        return carry

    lax.fori_loop(0, devices - 1, greet, 0)

    row = lax.broadcasted_iota(jnp.int32, (8, 128), 0)
    group = lax.broadcasted_iota(jnp.int32, (8, 128), 1) // 16
    tiles = ens_ref.shape[3] // 128

    state = []
    for m in range(0, 4, 2):
        start = tuple(tuple(ens_ref[m + k, f] for f in range(3)) for k in range(2))
        state.extend(
            lax.fori_loop(0, STEPS, lambda _, s: tuple(forecast_step(x) for x in s), start)
        )
    for f in range(3):
        for t in range(tiles):
            blocks = [
                swap_groups(state[m][f][:, 128 * t : 128 * t + 128], row, group) for m in range(4)
            ]
            for j, block in enumerate(swap_members(blocks, row)):
                send[8 * t + j, f] = block[0:4]
                send[8 * t + 4 + j, f] = block[4:8]

    recv[:, pl.ds(me, 1)] = send[me][:, None]
    pl.semaphore_wait(barrier, devices - 1)

    def scatter(i, carry):
        target, where = device_of(1 + lax.rem(i + 7, devices - 1))
        pltpu.make_async_remote_copy(
            src_ref=send.at[target],
            dst_ref=recv.at[:, me],
            send_sem=sems.at[0],
            recv_sem=sems.at[1],
            device_id=where,
            device_id_type=pl.DeviceIdType.MESH,
        ).start()
        return carry

    lax.fori_loop(0, devices - 1, scatter, 0)

    cells = 3 * 128
    picker = (lax.broadcasted_iota(jnp.int32, (cells, 128), 0) == cell_ref[...]).astype(jnp.float32)
    picker = picker.astype(jnp.bfloat16)
    obs_row = (lax.rem(cell_ref[...], 128) // PCOL).astype(jnp.float32)
    dist = (obs_row - 3.5) / 8.0
    weights = rinv_ref[...] * live_ref[...].astype(jnp.float32) * jnp.exp(-0.5 * dist * dist)
    square = (members, members)
    diagonal = lax.broadcasted_iota(jnp.int32, square, 0) == lax.broadcasted_iota(jnp.int32, square, 1)

    arrived = recv.at[:, pl.ds(0, devices - 1)]
    pltpu.make_async_copy(arrived, arrived, sems.at[1]).wait()

    states = jnp.concatenate([recv[f].reshape(members, 128) for f in range(3)], axis=1)
    centre = jnp.sum(states, axis=0, keepdims=True) * (1.0 / members)
    anomaly = states - centre
    high, low = halves(anomaly)
    c_high, c_low = halves(centre)
    c_rest = (centre - c_high.astype(jnp.float32) - c_low.astype(jnp.float32)).astype(jnp.bfloat16)
    centre_rows = jnp.concatenate([jnp.broadcast_to(c, (16, cells)) for c in (c_high, c_low, c_rest)], axis=0)
    picked = jnp.dot(
        jnp.concatenate([high, low, centre_rows], axis=0), picker, preferred_element_type=jnp.float32
    )
    seen = picked[:members] + picked[members : 2 * members]
    at = 2 * members
    seen_mean = picked[at : at + 1] + picked[at + 16 : at + 17] + picked[at + 32 : at + 33]
    innov = value_ref[...] - seen_mean
    weighted = seen * weights
    pushed = jnp.sum(weighted * innov, axis=1, keepdims=True)

    seen_high, seen_low = halves(seen)
    right = jnp.concatenate(
        [
            jnp.concatenate([seen_high, seen_high], axis=1),
            jnp.concatenate([seen_low, seen_low], axis=1),
        ],
        axis=0,
    )
    gram = lax.dot_general(
        left_of(weighted), right, (((1,), (1,)), ((), ())), preferred_element_type=jnp.float32
    )
    system = gram[:, :members] + gram[:, members:] + jnp.where(diagonal, (members - 1) / 1.1, 0.0)
    norm_c = jnp.max(jnp.sum(jnp.abs(system), axis=0, keepdims=True), axis=1, keepdims=True)
    root = system / norm_c
    eye15 = jnp.where(diagonal, 1.5, 0.0)
    factor = eye15 - 0.5 * root
    root = product(left_of(root), right_of(factor))
    inverse = factor
    for turn in range(1, NS_ITERS - 1):
        factor = eye15 - 0.5 * product(left_of(inverse), right_of(root))
        right = right_of(factor)
        root = product(left_of(root), right)
        inverse = product(left_of(inverse), right)
    left = left_of(inverse)
    last = left_of(eye15 - 0.5 * product(left, right_of(root)))
    ahead = jnp.concatenate([anomaly, jnp.broadcast_to(pushed, (members, 128))], axis=1)
    moved = product(last, right_of(product(left, right_of(ahead))))
    spread = moved[:, :cells]
    push = moved[:, cells:]
    scale = math.sqrt(members - 1) * lax.rsqrt(norm_c)
    for f in range(3):
        part = spread[:, 128 * f : 128 * f + 128]
        shift = centre[:, 128 * f : 128 * f + 128] + jnp.sum(part * push, axis=0, keepdims=True) / norm_c
        back_send[f] = (shift + scale * part).reshape(devices, 4, 128)

    back_recv[pl.ds(me, 1)] = back_send[:, pl.ds(me, 1)].reshape(1, 3, 4, 128)

    def give_back(i, carry):
        target, where = device_of(1 + lax.rem(i + 7, devices - 1))
        pltpu.make_async_remote_copy(
            src_ref=back_send.at[:, target],
            dst_ref=back_recv.at[me],
            send_sem=sems.at[2],
            recv_sem=sems.at[3],
            device_id=where,
            device_id_type=pl.DeviceIdType.MESH,
        ).start()
        return carry

    lax.fori_loop(0, devices - 1, give_back, 0)
    sent = send.at[pl.ds(0, devices - 1)]
    pltpu.make_async_copy(sent, sent, sems.at[0]).wait()
    arrived = back_recv.at[pl.ds(0, devices - 1)]
    pltpu.make_async_copy(arrived, arrived, sems.at[3]).wait()

    for f in range(3):
        for t in range(tiles):
            blocks = [
                jnp.concatenate([back_recv[8 * t + j, f], back_recv[8 * t + 4 + j, f]], axis=0)
                for j in range(4)
            ]
            for m, block in enumerate(swap_members(blocks, row)):
                out_ref[m, f, :, 128 * t : 128 * t + 128] = swap_groups(block, row, group)
    sent = back_send.at[:, pl.ds(0, devices - 1)]
    pltpu.make_async_copy(sent, sent, sems.at[2]).wait()


def one_strip(ensemble, obs_cell, obs_value, obs_rinv, obs_live):
    cores = lax.axis_size("group")
    devices = lax.axis_size("member") * cores
    vmem = pl.BlockSpec(memory_space=pltpu.VMEM)
    return pl.pallas_call(
        functools.partial(fused, devices, cores),
        out_shape=jax.ShapeDtypeStruct(ensemble.shape, jnp.float32),
        in_specs=[vmem] * 5,
        out_specs=vmem,
        scratch_shapes=[
            pltpu.VMEM((devices, 3, 4, 128), jnp.float32),
            pltpu.VMEM((3, devices, 4, 128), jnp.float32),
            pltpu.VMEM((3, devices, 4, 128), jnp.float32),
            pltpu.VMEM((devices, 3, 4, 128), jnp.float32),
            pltpu.SemaphoreType.DMA((4,)),
        ],
        compiler_params=pltpu.CompilerParams(collective_id=0, has_side_effects=True),
        name="fused",
    )(ensemble, obs_cell[0], obs_value[0], obs_rinv[0], obs_live[0])


def fits_one_strip(mesh):
    return mesh.shape["domain"] == 1


def solution(mesh):
    return jax.shard_map(
        one_strip if fits_one_strip(mesh) else local,
        mesh=mesh,
        in_specs=(
            P(("member", "group"), None, "domain", None),
            P("domain", ("member", "group"), None),
            P("domain", ("member", "group"), None),
            P("domain", ("member", "group"), None),
            P("domain", ("member", "group"), None),
        ),
        out_specs=P(("member", "group"), None, "domain", None),
        check_vma=False,
    )
```

```python
import functools
import math

import jax
import jax.numpy as jnp
from jax import lax
from jax.experimental import pallas as pl
from jax.experimental.pallas import tpu as pltpu
from jax.sharding import PartitionSpec as P

PCOL = 16
STEPS = 8
DEEP = 4
NS_ITERS = 5


HIGH = lax.Precision.HIGHEST


def with_halo(block, sides, width):
    for axis, dim in sides:
        count = lax.axis_size(axis)
        forward = [(i, i + 1) for i in range(count - 1)]
        backward = [(target, source) for source, target in forward]
        low = lax.ppermute(
            lax.slice_in_dim(block, block.shape[dim] - width, None, axis=dim), axis, forward
        )
        high = lax.ppermute(lax.slice_in_dim(block, 0, width, axis=dim), axis, backward)
        block = jnp.concatenate([low, block, high], axis=dim)
    return block


def split_parts(values):
    centre = values[:, 1:-1]
    north = values[:, 2:]
    south = values[:, :-2]
    east = jnp.roll(centre, -1, axis=-1)
    west = jnp.roll(centre, 1, axis=-1)
    return (
        0.25 * (north + south + east + west),
        0.5 * (east - west),
        0.5 * (north - south),
        centre,
    )


def advance(padded):
    height = padded[:, 0]
    speed_u = padded[:, 1]
    speed_v = padded[:, 2]
    depth = 1.0 + height
    h_avg, h_dx, h_dy, h_mid = split_parts(height)
    u_avg, u_dx, u_dy, u_mid = split_parts(speed_u)
    v_avg, v_dx, v_dy, v_mid = split_parts(speed_v)
    flux_x = split_parts(depth * speed_u)[1]
    flux_y = split_parts(depth * speed_v)[2]
    new_h = h_avg - 0.3 * (flux_x + flux_y)
    new_u = u_avg - 0.3 * (u_mid * u_dx + v_mid * u_dy + h_dx - 0.2 * v_mid)
    new_v = v_avg - 0.3 * (u_mid * v_dx + v_mid * v_dy + h_dy + 0.2 * u_mid)
    return jnp.stack([new_h, new_u, new_v], axis=1)


def local(ensemble, obs_cell, obs_value, obs_rinv, obs_live):
    physical_fields_vector = ensemble
    mem_local = physical_fields_vector.shape[0]
    rows = physical_fields_vector.shape[2]
    width_x = physical_fields_vector.shape[3]
    strip = lax.axis_index("domain")
    total_rows = rows * lax.axis_size("domain")
    for block_index in range(STEPS // DEEP):
        padded = with_halo(physical_fields_vector, (("domain", 2),), DEEP)
        for sub_index in range(DEEP):
            padded = advance(padded)
            if sub_index + 1 < DEEP:
                margin = DEEP - 1 - sub_index
                global_row = strip * rows - margin + jnp.arange(padded.shape[2])
                inside = (global_row >= 0) & (global_row < total_rows)
                padded = jnp.where(inside[None, None, :, None], padded, 0.0)
        physical_fields_vector = padded
    domain_pieces = width_x // PCOL
    cells = 3 * rows * PCOL
    pieces = (
        physical_fields_vector.reshape(mem_local, 3, rows, domain_pieces, PCOL)
        .transpose(0, 3, 1, 2, 4)
        .reshape(mem_local, domain_pieces, cells)
    )
    gathered = lax.all_to_all(pieces, ("member", "group"), split_axis=1, concat_axis=0, tiled=True)
    members = gathered.reshape(-1, cells)
    ensemble_size = members.shape[0]
    centre_row = jnp.mean(members, axis=0)
    anomaly = members - centre_row
    picker = (obs_cell[0, 0][None, :] == jnp.arange(cells)[:, None]).astype(jnp.float32)
    seen = jnp.dot(anomaly, picker, precision=HIGH)
    seen_mean = jnp.dot(centre_row[None, :], picker, precision=HIGH)[0]
    innov = obs_value[0, 0] - seen_mean
    weight = obs_rinv[0, 0] * obs_live[0, 0].astype(jnp.float32)
    obs_row = (obs_cell[0, 0] % (rows * PCOL) // PCOL).astype(jnp.float32)
    packed = jnp.concatenate([seen, innov[None, :], weight[None, :], obs_row[None, :]], axis=0)[
        :, None, :
    ]
    nearby = with_halo(packed, (("domain", 1),), 1)
    slots = packed.shape[2]
    nearby = nearby.reshape(ensemble_size + 3, 3 * slots)
    offset = (jnp.arange(3 * slots) // slots - 1).astype(jnp.float32)
    dist_y = offset * rows + nearby[ensemble_size + 2] - 0.5 * (rows - 1)
    taper = jnp.exp(-0.5 * (dist_y / rows) * (dist_y / rows))
    weights = nearby[ensemble_size + 1] * taper
    seen_all = nearby[:ensemble_size]
    gram = jnp.dot(seen_all * weights[None, :], seen_all.T, precision=HIGH)
    ident = jnp.eye(ensemble_size, dtype=jnp.float32)
    system = (ensemble_size - 1) / 1.1 * ident + gram
    norm_c = jnp.max(jnp.sum(jnp.abs(system), axis=1))
    root_m = system / norm_c
    inverse = ident
    for turn_index in range(NS_ITERS):
        factor = 1.5 * ident - 0.5 * jnp.dot(inverse, root_m, precision=HIGH)
        if turn_index + 1 < NS_ITERS:
            root_m = jnp.dot(root_m, factor, precision=HIGH)
        inverse = jnp.dot(factor, inverse, precision=HIGH)
    inverse = inverse / jnp.sqrt(norm_c)
    pushed = jnp.dot(seen_all, weights * nearby[ensemble_size], precision=HIGH)
    shift_w = jnp.dot(inverse, jnp.dot(inverse, pushed, precision=HIGH), precision=HIGH)
    mixing = math.sqrt(ensemble_size - 1) * inverse + shift_w[:, None]
    result = centre_row + lax.dot_general(mixing, anomaly, (((0,), (0,)), ((), ())), precision=HIGH)
    returned = lax.all_to_all(
        result.reshape(ensemble_size, 1, cells),
        ("member", "group"),
        split_axis=0,
        concat_axis=1,
        tiled=True,
    )
    return (
        returned.reshape(mem_local, domain_pieces, 3, rows, PCOL)
        .transpose(0, 2, 3, 1, 4)
        .reshape(mem_local, 3, rows, width_x)
    )


def swap_groups(x, row, group):
    for d in (4, 2, 1):
        row_bit = (row // d) % 2
        group_bit = (group // d) % 2
        up = pltpu.roll(pltpu.roll(x, 8 - d, 0), 16 * d, 1)
        if d == 4:
            other = up
        else:
            down = pltpu.roll(pltpu.roll(x, d, 0), 128 - 16 * d, 1)
            other = jnp.where(group_bit == 1, up, down)
        x = jnp.where(row_bit == group_bit, x, other)
    return x


def swap_members(blocks, row):
    blocks = list(blocks)
    for d in (2, 1):
        low = (row // d) % 2 == 0
        for i in range(4):
            if (i // d) % 2 == 0:
                a, b = blocks[i], blocks[i + d]
                blocks[i] = jnp.where(low, a, pltpu.roll(b, d, 0))
                blocks[i + d] = jnp.where(low, pltpu.roll(a, 8 - d, 0), b)
    return blocks


def forecast_step(fields):
    h, u, v = fields
    width = h.shape[1]
    row = lax.broadcasted_iota(jnp.int32, h.shape, 0)
    first, last = row == 0, row == h.shape[0] - 1

    def around(x):
        return (
            pltpu.roll(x, width - 1, 1),
            pltpu.roll(x, 1, 1),
            jnp.where(last, 0.0, pltpu.roll(x, x.shape[0] - 1, 0)),
            jnp.where(first, 0.0, pltpu.roll(x, 1, 0)),
        )

    he, hw, hn, hs = around(h)
    ue, uw, un, us = around(u)
    ve, vw, vn, vs = around(v)
    flux = ((1.0 + he) * ue - (1.0 + hw) * uw) + ((1.0 + hn) * vn - (1.0 + hs) * vs)
    new_h = 0.25 * ((hn + hs) + (he + hw)) - 0.15 * flux
    new_u = 0.25 * ((un + us) + (ue + uw)) - 0.15 * (u * (ue - uw) + v * (un - us) + (he - hw)) + 0.06 * v
    new_v = 0.25 * ((vn + vs) + (ve + vw)) - 0.15 * (u * (ve - vw) + v * (vn - vs) + (hn - hs)) - 0.06 * u
    return new_h, new_u, new_v


def halves(x):
    hi = x.astype(jnp.bfloat16)
    lo = (x - hi.astype(jnp.float32)).astype(jnp.bfloat16)
    return hi, lo


def left_of(x):
    return jnp.concatenate(halves(x), axis=1)


def right_of(x):
    wide = jnp.concatenate(halves(x), axis=1)
    return jnp.concatenate([wide, wide], axis=0)


def product(left, right):
    both = jnp.dot(left, right, preferred_element_type=jnp.float32)
    half = both.shape[1] // 2
    return both[:, :half] + both[:, half:]


def fused(
    devices,
    cores,
    ens_ref,
    cell_ref,
    value_ref,
    rinv_ref,
    live_ref,
    out_ref,
    send,
    recv,
    back_send,
    back_recv,
    sems,
):
    members = devices * 4
    me = lax.axis_index("member") * cores + lax.axis_index("group")

    def device_of(k):
        target = lax.rem(me + k, devices)
        return target, {"member": target // cores, "group": lax.rem(target, cores)}

    def each_other(send_to):
        if devices != 32:

            def step(i, carry):
                send_to(*device_of(i + 1))
                return carry

            lax.fori_loop(0, devices - 1, step, 0)
            return
        plane, seat = me // 8, lax.rem(me, 8)
        upper = plane // 2
        order = (
            3 - 3 * upper,
            2 - upper,
            2 * upper + 1 - lax.rem(plane, 2),
            plane,
        )
        for position, there in enumerate(order):

            def step(i, carry):
                target = there * 8 + lax.rem(seat + i, 8)
                where = {"member": target // cores, "group": lax.rem(target, cores)}
                send_to(target, where)
                return carry

            lax.fori_loop(1 if position == 3 else 0, 8, step, 0)

    barrier = pltpu.get_barrier_semaphore()

    def greet(i, carry):
        _, where = device_of(i + 1)
        pl.semaphore_signal(barrier, inc=1, device_id=where, device_id_type=pl.DeviceIdType.MESH)
        return carry

    lax.fori_loop(0, devices - 1, greet, 0)

    row = lax.broadcasted_iota(jnp.int32, (8, 128), 0)
    group = lax.broadcasted_iota(jnp.int32, (8, 128), 1) // 16
    tiles = ens_ref.shape[3] // 128

    state = []
    for m in range(0, 4, 2):
        start = tuple(tuple(ens_ref[m + k, f] for f in range(3)) for k in range(2))
        state.extend(
            lax.fori_loop(0, STEPS, lambda _, s: tuple(forecast_step(x) for x in s), start)
        )
    for f in range(3):
        for t in range(tiles):
            blocks = [
                swap_groups(state[m][f][:, 128 * t : 128 * t + 128], row, group) for m in range(4)
            ]
            for j, block in enumerate(swap_members(blocks, row)):
                send[8 * t + j, f] = block[0:4]
                send[8 * t + 4 + j, f] = block[4:8]

    recv[pl.ds(me, 1)] = send[pl.ds(me, 1)]
    pl.semaphore_wait(barrier, devices - 1)

    def scatter(target, where):
        pltpu.make_async_remote_copy(
            src_ref=send.at[target],
            dst_ref=recv.at[me],
            send_sem=sems.at[0],
            recv_sem=sems.at[1],
            device_id=where,
            device_id_type=pl.DeviceIdType.MESH,
        ).start()

    each_other(scatter)

    cells = 3 * 128
    picker = (lax.broadcasted_iota(jnp.int32, (cells, 128), 0) == cell_ref[...]).astype(jnp.float32)
    picker = picker.astype(jnp.bfloat16)
    obs_row = (lax.rem(cell_ref[...], 128) // PCOL).astype(jnp.float32)
    dist = (obs_row - 3.5) / 8.0
    weights = rinv_ref[...] * live_ref[...].astype(jnp.float32) * jnp.exp(-0.5 * dist * dist)
    square = (members, members)
    diagonal = lax.broadcasted_iota(jnp.int32, square, 0) == lax.broadcasted_iota(jnp.int32, square, 1)

    arrived = recv.at[pl.ds(0, devices - 1)]
    pltpu.make_async_copy(arrived, arrived, sems.at[1]).wait()

    states = jnp.concatenate([recv[:, f].reshape(members, 128) for f in range(3)], axis=1)
    centre = jnp.sum(states, axis=0, keepdims=True) * (1.0 / members)
    anomaly = states - centre
    high, low = halves(anomaly)
    c_high, c_low = halves(centre)
    c_rest = (centre - c_high.astype(jnp.float32) - c_low.astype(jnp.float32)).astype(jnp.bfloat16)
    centre_rows = jnp.concatenate([jnp.broadcast_to(c, (16, cells)) for c in (c_high, c_low, c_rest)], axis=0)
    picked = jnp.dot(
        jnp.concatenate([high, low, centre_rows], axis=0), picker, preferred_element_type=jnp.float32
    )
    seen = picked[:members] + picked[members : 2 * members]
    at = 2 * members
    seen_mean = picked[at : at + 1] + picked[at + 16 : at + 17] + picked[at + 32 : at + 33]
    innov = value_ref[...] - seen_mean
    weighted = seen * weights
    pushed = jnp.sum(weighted * innov, axis=1, keepdims=True)

    seen_high, seen_low = halves(seen)
    right = jnp.concatenate(
        [
            jnp.concatenate([seen_high, seen_high], axis=1),
            jnp.concatenate([seen_low, seen_low], axis=1),
        ],
        axis=0,
    )
    gram = lax.dot_general(
        left_of(weighted), right, (((1,), (1,)), ((), ())), preferred_element_type=jnp.float32
    )
    system = gram[:, :members] + gram[:, members:] + jnp.where(diagonal, (members - 1) / 1.1, 0.0)
    norm_c = jnp.max(jnp.sum(jnp.abs(system), axis=0, keepdims=True), axis=1, keepdims=True)
    root = system / norm_c
    eye15 = jnp.where(diagonal, 1.5, 0.0)
    factor = eye15 - 0.5 * root
    root = product(left_of(root), right_of(factor))
    inverse = factor
    for turn in range(1, NS_ITERS - 1):
        factor = eye15 - 0.5 * product(left_of(inverse), right_of(root))
        right = right_of(factor)
        root = product(left_of(root), right)
        inverse = product(left_of(inverse), right)
    left = left_of(inverse)
    last = left_of(eye15 - 0.5 * product(left, right_of(root)))
    ahead = jnp.concatenate([anomaly, jnp.broadcast_to(pushed, (members, 128))], axis=1)
    moved = product(last, right_of(product(left, right_of(ahead))))
    spread = moved[:, :cells]
    push = moved[:, cells:]
    scale = math.sqrt(members - 1) * lax.rsqrt(norm_c)
    for f in range(3):
        part = spread[:, 128 * f : 128 * f + 128]
        shift = centre[:, 128 * f : 128 * f + 128] + jnp.sum(part * push, axis=0, keepdims=True) / norm_c
        back_send[:, f] = (shift + scale * part).reshape(devices, 4, 128)

    back_recv[pl.ds(me, 1)] = back_send[pl.ds(me, 1)]

    def give_back(target, where):
        pltpu.make_async_remote_copy(
            src_ref=back_send.at[target],
            dst_ref=back_recv.at[me],
            send_sem=sems.at[2],
            recv_sem=sems.at[3],
            device_id=where,
            device_id_type=pl.DeviceIdType.MESH,
        ).start()

    each_other(give_back)
    sent = send.at[pl.ds(0, devices - 1)]
    pltpu.make_async_copy(sent, sent, sems.at[0]).wait()
    arrived = back_recv.at[pl.ds(0, devices - 1)]
    pltpu.make_async_copy(arrived, arrived, sems.at[3]).wait()

    out_ref[...] = back_recv[...]
    sent = back_send.at[pl.ds(0, devices - 1)]
    pltpu.make_async_copy(sent, sent, sems.at[2]).wait()


def lay_out(back_ref, out_ref):
    row = lax.broadcasted_iota(jnp.int32, (8, 128), 0)
    group = lax.broadcasted_iota(jnp.int32, (8, 128), 1) // 16
    tiles = out_ref.shape[3] // 128
    for f in range(3):
        for t in range(tiles):
            blocks = [
                jnp.concatenate([back_ref[8 * t + j, f], back_ref[8 * t + 4 + j, f]], axis=0)
                for j in range(4)
            ]
            for m, block in enumerate(swap_members(blocks, row)):
                out_ref[m, f, :, 128 * t : 128 * t + 128] = swap_groups(block, row, group)


def one_strip(ensemble, obs_cell, obs_value, obs_rinv, obs_live):
    cores = lax.axis_size("group")
    devices = lax.axis_size("member") * cores
    vmem = pl.BlockSpec(memory_space=pltpu.VMEM)
    pieces = pl.pallas_call(
        functools.partial(fused, devices, cores),
        out_shape=pltpu.VMEM((devices, 3, 4, 128), jnp.float32),
        in_specs=[vmem] * 5,
        out_specs=vmem,
        scratch_shapes=[
            pltpu.VMEM((devices, 3, 4, 128), jnp.float32),
            pltpu.VMEM((devices, 3, 4, 128), jnp.float32),
            pltpu.VMEM((devices, 3, 4, 128), jnp.float32),
            pltpu.VMEM((devices, 3, 4, 128), jnp.float32),
            pltpu.SemaphoreType.DMA((4,)),
        ],
        compiler_params=pltpu.CompilerParams(collective_id=0, has_side_effects=True),
        name="fused",
    )(ensemble, obs_cell[0], obs_value[0], obs_rinv[0], obs_live[0])
    return pl.pallas_call(
        lay_out,
        out_shape=jax.ShapeDtypeStruct(ensemble.shape, jnp.float32),
        in_specs=[vmem],
        out_specs=vmem,
        name="lay_out",
    )(pltpu.with_memory_space_constraint(pieces, pltpu.VMEM))


def fits_one_strip(mesh):
    return mesh.shape["domain"] == 1


def solution(mesh):
    return jax.shard_map(
        one_strip if fits_one_strip(mesh) else local,
        mesh=mesh,
        in_specs=(
            P(("member", "group"), None, "domain", None),
            P("domain", ("member", "group"), None),
            P("domain", ("member", "group"), None),
            P("domain", ("member", "group"), None),
            P("domain", ("member", "group"), None),
        ),
        out_specs=P(("member", "group"), None, "domain", None),
        check_vma=False,
    )
```

```python
import functools
import math

import jax
import jax.numpy as jnp
from jax import lax
from jax.experimental import pallas as pl
from jax.experimental.pallas import tpu as pltpu
from jax.sharding import PartitionSpec as P

PCOL = 16
STEPS = 8
DEEP = 4
NS_ITERS = 5


HIGH = lax.Precision.HIGHEST


def with_halo(block, sides, width):
    for axis, dim in sides:
        count = lax.axis_size(axis)
        forward = [(i, i + 1) for i in range(count - 1)]
        backward = [(target, source) for source, target in forward]
        low = lax.ppermute(
            lax.slice_in_dim(block, block.shape[dim] - width, None, axis=dim), axis, forward
        )
        high = lax.ppermute(lax.slice_in_dim(block, 0, width, axis=dim), axis, backward)
        block = jnp.concatenate([low, block, high], axis=dim)
    return block


def split_parts(values):
    centre = values[:, 1:-1]
    north = values[:, 2:]
    south = values[:, :-2]
    east = jnp.roll(centre, -1, axis=-1)
    west = jnp.roll(centre, 1, axis=-1)
    return (
        0.25 * (north + south + east + west),
        0.5 * (east - west),
        0.5 * (north - south),
        centre,
    )


def advance(padded):
    height = padded[:, 0]
    speed_u = padded[:, 1]
    speed_v = padded[:, 2]
    depth = 1.0 + height
    h_avg, h_dx, h_dy, h_mid = split_parts(height)
    u_avg, u_dx, u_dy, u_mid = split_parts(speed_u)
    v_avg, v_dx, v_dy, v_mid = split_parts(speed_v)
    flux_x = split_parts(depth * speed_u)[1]
    flux_y = split_parts(depth * speed_v)[2]
    new_h = h_avg - 0.3 * (flux_x + flux_y)
    new_u = u_avg - 0.3 * (u_mid * u_dx + v_mid * u_dy + h_dx - 0.2 * v_mid)
    new_v = v_avg - 0.3 * (u_mid * v_dx + v_mid * v_dy + h_dy + 0.2 * u_mid)
    return jnp.stack([new_h, new_u, new_v], axis=1)


def local(ensemble, obs_cell, obs_value, obs_rinv, obs_live):
    physical_fields_vector = ensemble
    mem_local = physical_fields_vector.shape[0]
    rows = physical_fields_vector.shape[2]
    width_x = physical_fields_vector.shape[3]
    strip = lax.axis_index("domain")
    total_rows = rows * lax.axis_size("domain")
    for block_index in range(STEPS // DEEP):
        padded = with_halo(physical_fields_vector, (("domain", 2),), DEEP)
        for sub_index in range(DEEP):
            padded = advance(padded)
            if sub_index + 1 < DEEP:
                margin = DEEP - 1 - sub_index
                global_row = strip * rows - margin + jnp.arange(padded.shape[2])
                inside = (global_row >= 0) & (global_row < total_rows)
                padded = jnp.where(inside[None, None, :, None], padded, 0.0)
        physical_fields_vector = padded
    domain_pieces = width_x // PCOL
    cells = 3 * rows * PCOL
    pieces = (
        physical_fields_vector.reshape(mem_local, 3, rows, domain_pieces, PCOL)
        .transpose(0, 3, 1, 2, 4)
        .reshape(mem_local, domain_pieces, cells)
    )
    gathered = lax.all_to_all(pieces, ("member", "group"), split_axis=1, concat_axis=0, tiled=True)
    members = gathered.reshape(-1, cells)
    ensemble_size = members.shape[0]
    centre_row = jnp.mean(members, axis=0)
    anomaly = members - centre_row
    picker = (obs_cell[0, 0][None, :] == jnp.arange(cells)[:, None]).astype(jnp.float32)
    seen = jnp.dot(anomaly, picker, precision=HIGH)
    seen_mean = jnp.dot(centre_row[None, :], picker, precision=HIGH)[0]
    innov = obs_value[0, 0] - seen_mean
    weight = obs_rinv[0, 0] * obs_live[0, 0].astype(jnp.float32)
    obs_row = (obs_cell[0, 0] % (rows * PCOL) // PCOL).astype(jnp.float32)
    packed = jnp.concatenate([seen, innov[None, :], weight[None, :], obs_row[None, :]], axis=0)[
        :, None, :
    ]
    nearby = with_halo(packed, (("domain", 1),), 1)
    slots = packed.shape[2]
    nearby = nearby.reshape(ensemble_size + 3, 3 * slots)
    offset = (jnp.arange(3 * slots) // slots - 1).astype(jnp.float32)
    dist_y = offset * rows + nearby[ensemble_size + 2] - 0.5 * (rows - 1)
    taper = jnp.exp(-0.5 * (dist_y / rows) * (dist_y / rows))
    weights = nearby[ensemble_size + 1] * taper
    seen_all = nearby[:ensemble_size]
    gram = jnp.dot(seen_all * weights[None, :], seen_all.T, precision=HIGH)
    ident = jnp.eye(ensemble_size, dtype=jnp.float32)
    system = (ensemble_size - 1) / 1.1 * ident + gram
    norm_c = jnp.max(jnp.sum(jnp.abs(system), axis=1))
    root_m = system / norm_c
    inverse = ident
    for turn_index in range(NS_ITERS):
        factor = 1.5 * ident - 0.5 * jnp.dot(inverse, root_m, precision=HIGH)
        if turn_index + 1 < NS_ITERS:
            root_m = jnp.dot(root_m, factor, precision=HIGH)
        inverse = jnp.dot(factor, inverse, precision=HIGH)
    inverse = inverse / jnp.sqrt(norm_c)
    pushed = jnp.dot(seen_all, weights * nearby[ensemble_size], precision=HIGH)
    shift_w = jnp.dot(inverse, jnp.dot(inverse, pushed, precision=HIGH), precision=HIGH)
    mixing = math.sqrt(ensemble_size - 1) * inverse + shift_w[:, None]
    result = centre_row + lax.dot_general(mixing, anomaly, (((0,), (0,)), ((), ())), precision=HIGH)
    returned = lax.all_to_all(
        result.reshape(ensemble_size, 1, cells),
        ("member", "group"),
        split_axis=0,
        concat_axis=1,
        tiled=True,
    )
    return (
        returned.reshape(mem_local, domain_pieces, 3, rows, PCOL)
        .transpose(0, 2, 3, 1, 4)
        .reshape(mem_local, 3, rows, width_x)
    )


def swap_groups(x, row, group):
    for d in (4, 2, 1):
        row_bit = (row // d) % 2
        group_bit = (group // d) % 2
        up = pltpu.roll(pltpu.roll(x, 8 - d, 0), 16 * d, 1)
        if d == 4:
            other = up
        else:
            down = pltpu.roll(pltpu.roll(x, d, 0), 128 - 16 * d, 1)
            other = jnp.where(group_bit == 1, up, down)
        x = jnp.where(row_bit == group_bit, x, other)
    return x


def swap_members(blocks, row):
    blocks = list(blocks)
    for d in (2, 1):
        low = (row // d) % 2 == 0
        for i in range(4):
            if (i // d) % 2 == 0:
                a, b = blocks[i], blocks[i + d]
                blocks[i] = jnp.where(low, a, pltpu.roll(b, d, 0))
                blocks[i + d] = jnp.where(low, pltpu.roll(a, 8 - d, 0), b)
    return blocks


def forecast_step(fields):
    h, u, v = fields
    width = h.shape[1]
    row = lax.broadcasted_iota(jnp.int32, h.shape, 0)
    first, last = row == 0, row == h.shape[0] - 1

    def around(x):
        return (
            pltpu.roll(x, width - 1, 1),
            pltpu.roll(x, 1, 1),
            jnp.where(last, 0.0, pltpu.roll(x, x.shape[0] - 1, 0)),
            jnp.where(first, 0.0, pltpu.roll(x, 1, 0)),
        )

    he, hw, hn, hs = around(h)
    ue, uw, un, us = around(u)
    ve, vw, vn, vs = around(v)
    flux = ((1.0 + he) * ue - (1.0 + hw) * uw) + ((1.0 + hn) * vn - (1.0 + hs) * vs)
    new_h = 0.25 * ((hn + hs) + (he + hw)) - 0.15 * flux
    new_u = 0.25 * ((un + us) + (ue + uw)) - 0.15 * (u * (ue - uw) + v * (un - us) + (he - hw)) + 0.06 * v
    new_v = 0.25 * ((vn + vs) + (ve + vw)) - 0.15 * (u * (ve - vw) + v * (vn - vs) + (hn - hs)) - 0.06 * u
    return new_h, new_u, new_v


def halves(x):
    hi = x.astype(jnp.bfloat16)
    lo = (x - hi.astype(jnp.float32)).astype(jnp.bfloat16)
    return hi, lo


def left_of(x):
    return jnp.concatenate(halves(x), axis=1)


def right_of(x):
    wide = jnp.concatenate(halves(x), axis=1)
    return jnp.concatenate([wide, wide], axis=0)


def product(left, right):
    both = jnp.dot(left, right, preferred_element_type=jnp.float32)
    half = both.shape[1] // 2
    return both[:, :half] + both[:, half:]


def fused(
    devices,
    cores,
    ens_hbm,
    cell_hbm,
    value_hbm,
    rinv_hbm,
    live_hbm,
    out_ref,
    ens_ref,
    cell_ref,
    value_ref,
    rinv_ref,
    live_ref,
    load_sems,
    send,
    recv,
    back_send,
    back_recv,
    sems,
):
    members = devices * 4
    me = lax.axis_index("member") * cores + lax.axis_index("group")

    def device_of(k):
        target = lax.rem(me + k, devices)
        return target, {"member": target // cores, "group": lax.rem(target, cores)}

    def each_other(send_to):
        if devices != 32:

            def step(i, carry):
                send_to(*device_of(i + 1))
                return carry

            lax.fori_loop(0, devices - 1, step, 0)
            return
        plane, seat = me // 8, lax.rem(me, 8)
        upper = plane // 2
        order = (
            3 - 3 * upper,
            2 - upper,
            2 * upper + 1 - lax.rem(plane, 2),
            plane,
        )
        for position, there in enumerate(order):

            def step(i, carry):
                target = there * 8 + lax.rem(seat + i, 8)
                where = {"member": target // cores, "group": lax.rem(target, cores)}
                send_to(target, where)
                return carry

            lax.fori_loop(1 if position == 3 else 0, 8, step, 0)

    pairs = (
        (ens_hbm, ens_ref),
        (cell_hbm, cell_ref),
        (value_hbm, value_ref),
        (rinv_hbm, rinv_ref),
        (live_hbm, live_ref),
    )
    loads = [pltpu.make_async_copy(a, b, load_sems.at[i]) for i, (a, b) in enumerate(pairs)]
    for load in loads:
        load.start()

    barrier = pltpu.get_barrier_semaphore()

    def greet(i, carry):
        _, where = device_of(i + 1)
        pl.semaphore_signal(barrier, inc=1, device_id=where, device_id_type=pl.DeviceIdType.MESH)
        return carry

    lax.fori_loop(0, devices - 1, greet, 0)
    loads[0].wait()

    row = lax.broadcasted_iota(jnp.int32, (8, 128), 0)
    group = lax.broadcasted_iota(jnp.int32, (8, 128), 1) // 16
    tiles = ens_ref.shape[3] // 128

    state = []
    for m in range(0, 4, 2):
        start = tuple(tuple(ens_ref[m + k, f] for f in range(3)) for k in range(2))
        state.extend(
            lax.fori_loop(0, STEPS, lambda _, s: tuple(forecast_step(x) for x in s), start)
        )
    for f in range(3):
        for t in range(tiles):
            blocks = [
                swap_groups(state[m][f][:, 128 * t : 128 * t + 128], row, group) for m in range(4)
            ]
            for j, block in enumerate(swap_members(blocks, row)):
                send[8 * t + j, f] = block[0:4]
                send[8 * t + 4 + j, f] = block[4:8]

    recv[pl.ds(me, 1)] = send[pl.ds(me, 1)]
    pl.semaphore_wait(barrier, devices - 1)

    def scatter(target, where):
        pltpu.make_async_remote_copy(
            src_ref=send.at[target],
            dst_ref=recv.at[me],
            send_sem=sems.at[0],
            recv_sem=sems.at[1],
            device_id=where,
            device_id_type=pl.DeviceIdType.MESH,
        ).start()

    each_other(scatter)

    for load in loads[1:]:
        load.wait()
    cells = 3 * 128
    picker = (lax.broadcasted_iota(jnp.int32, (cells, 128), 0) == cell_ref[...]).astype(jnp.float32)
    picker = picker.astype(jnp.bfloat16)
    obs_row = (lax.rem(cell_ref[...], 128) // PCOL).astype(jnp.float32)
    dist = (obs_row - 3.5) / 8.0
    weights = rinv_ref[...] * live_ref[...].astype(jnp.float32) * jnp.exp(-0.5 * dist * dist)
    square = (members, members)
    diagonal = lax.broadcasted_iota(jnp.int32, square, 0) == lax.broadcasted_iota(jnp.int32, square, 1)

    arrived = recv.at[pl.ds(0, devices - 1)]
    pltpu.make_async_copy(arrived, arrived, sems.at[1]).wait()

    states = jnp.concatenate([recv[:, f].reshape(members, 128) for f in range(3)], axis=1)
    centre = jnp.sum(states, axis=0, keepdims=True) * (1.0 / members)
    anomaly = states - centre
    high, low = halves(anomaly)
    c_high, c_low = halves(centre)
    c_rest = (centre - c_high.astype(jnp.float32) - c_low.astype(jnp.float32)).astype(jnp.bfloat16)
    centre_rows = jnp.concatenate([jnp.broadcast_to(c, (16, cells)) for c in (c_high, c_low, c_rest)], axis=0)
    picked = jnp.dot(
        jnp.concatenate([high, low, centre_rows], axis=0), picker, preferred_element_type=jnp.float32
    )
    seen = picked[:members] + picked[members : 2 * members]
    at = 2 * members
    seen_mean = picked[at : at + 1] + picked[at + 16 : at + 17] + picked[at + 32 : at + 33]
    innov = value_ref[...] - seen_mean
    weighted = seen * weights
    pushed = jnp.sum(weighted * innov, axis=1, keepdims=True)

    seen_high, seen_low = halves(seen)
    right = jnp.concatenate(
        [
            jnp.concatenate([seen_high, seen_high], axis=1),
            jnp.concatenate([seen_low, seen_low], axis=1),
        ],
        axis=0,
    )
    gram = lax.dot_general(
        left_of(weighted), right, (((1,), (1,)), ((), ())), preferred_element_type=jnp.float32
    )
    system = gram[:, :members] + gram[:, members:] + jnp.where(diagonal, (members - 1) / 1.1, 0.0)
    norm_c = jnp.max(jnp.sum(jnp.abs(system), axis=0, keepdims=True), axis=1, keepdims=True)
    root = system / norm_c
    eye15 = jnp.where(diagonal, 1.5, 0.0)
    factor = eye15 - 0.5 * root
    root = product(left_of(root), right_of(factor))
    inverse = factor
    for turn in range(1, NS_ITERS - 1):
        factor = eye15 - 0.5 * product(left_of(inverse), right_of(root))
        right = right_of(factor)
        root = product(left_of(root), right)
        inverse = product(left_of(inverse), right)
    left = left_of(inverse)
    last = left_of(eye15 - 0.5 * product(left, right_of(root)))
    ahead = jnp.concatenate([anomaly, jnp.broadcast_to(pushed, (members, 128))], axis=1)
    moved = product(last, right_of(product(left, right_of(ahead))))
    spread = moved[:, :cells]
    push = moved[:, cells:]
    scale = math.sqrt(members - 1) * lax.rsqrt(norm_c)
    for f in range(3):
        part = spread[:, 128 * f : 128 * f + 128]
        shift = centre[:, 128 * f : 128 * f + 128] + jnp.sum(part * push, axis=0, keepdims=True) / norm_c
        back_send[:, f] = (shift + scale * part).reshape(devices, 4, 128)

    back_recv[pl.ds(me, 1)] = back_send[pl.ds(me, 1)]

    def give_back(target, where):
        pltpu.make_async_remote_copy(
            src_ref=back_send.at[target],
            dst_ref=back_recv.at[me],
            send_sem=sems.at[2],
            recv_sem=sems.at[3],
            device_id=where,
            device_id_type=pl.DeviceIdType.MESH,
        ).start()

    each_other(give_back)
    sent = send.at[pl.ds(0, devices - 1)]
    pltpu.make_async_copy(sent, sent, sems.at[0]).wait()
    arrived = back_recv.at[pl.ds(0, devices - 1)]
    pltpu.make_async_copy(arrived, arrived, sems.at[3]).wait()

    out_ref[...] = back_recv[...]
    sent = back_send.at[pl.ds(0, devices - 1)]
    pltpu.make_async_copy(sent, sent, sems.at[2]).wait()


def lay_out(back_ref, out_ref):
    row = lax.broadcasted_iota(jnp.int32, (8, 128), 0)
    group = lax.broadcasted_iota(jnp.int32, (8, 128), 1) // 16
    tiles = out_ref.shape[3] // 128
    for f in range(3):
        for t in range(tiles):
            blocks = [
                jnp.concatenate([back_ref[8 * t + j, f], back_ref[8 * t + 4 + j, f]], axis=0)
                for j in range(4)
            ]
            for m, block in enumerate(swap_members(blocks, row)):
                out_ref[m, f, :, 128 * t : 128 * t + 128] = swap_groups(block, row, group)


def one_strip(ensemble, obs_cell, obs_value, obs_rinv, obs_live):
    cores = lax.axis_size("group")
    devices = lax.axis_size("member") * cores
    vmem = pl.BlockSpec(memory_space=pltpu.VMEM)
    pieces = pl.pallas_call(
        functools.partial(fused, devices, cores),
        out_shape=pltpu.VMEM((devices, 3, 4, 128), jnp.float32),
        in_specs=[pl.BlockSpec(memory_space=pltpu.HBM)] * 5,
        out_specs=vmem,
        scratch_shapes=[
            pltpu.VMEM(ensemble.shape, jnp.float32),
            pltpu.VMEM(obs_cell.shape[1:], jnp.int32),
            pltpu.VMEM(obs_value.shape[1:], jnp.float32),
            pltpu.VMEM(obs_rinv.shape[1:], jnp.float32),
            pltpu.VMEM(obs_live.shape[1:], jnp.int32),
            pltpu.SemaphoreType.DMA((5,)),
            pltpu.VMEM((devices, 3, 4, 128), jnp.float32),
            pltpu.VMEM((devices, 3, 4, 128), jnp.float32),
            pltpu.VMEM((devices, 3, 4, 128), jnp.float32),
            pltpu.VMEM((devices, 3, 4, 128), jnp.float32),
            pltpu.SemaphoreType.DMA((4,)),
        ],
        compiler_params=pltpu.CompilerParams(collective_id=0, has_side_effects=True),
        name="fused",
    )(ensemble, obs_cell[0], obs_value[0], obs_rinv[0], obs_live[0])
    return pl.pallas_call(
        lay_out,
        out_shape=jax.ShapeDtypeStruct(ensemble.shape, jnp.float32),
        in_specs=[vmem],
        out_specs=vmem,
        name="lay_out",
    )(pltpu.with_memory_space_constraint(pieces, pltpu.VMEM))


def fits_one_strip(mesh):
    return mesh.shape["domain"] == 1


def solution(mesh):
    return jax.shard_map(
        one_strip if fits_one_strip(mesh) else local,
        mesh=mesh,
        in_specs=(
            P(("member", "group"), None, "domain", None),
            P("domain", ("member", "group"), None),
            P("domain", ("member", "group"), None),
            P("domain", ("member", "group"), None),
            P("domain", ("member", "group"), None),
        ),
        out_specs=P(("member", "group"), None, "domain", None),
        check_vma=False,
    )
```
